32 devices in a mesh: uly: 2 (over x), blk: 8 (over z, y), dp: 2 (over core).
Axes of the slice: x: 2, y: 2, z: 4, core: 2. Of those that a mesh axis runs over, the one named last changes fastest.
Arguments:
- queries: bfloat16 [2, 2048, 1024], P('dp', ('blk', 'uly')), may hold values from -6 to 6
- out_grad: bfloat16 [2, 2048, 1024], P('dp', ('blk', 'uly')), may hold values from -6 to 6
- keys_values: bfloat16 [2, 2048, 256], P('dp', ('blk', 'uly')), may hold values from -9 to 9
- attn_output: bfloat16 [2, 8, 2048, 128], P('dp', 'uly', 'blk'), may hold values from -6 to 6
- logsumexp: float32 [2, 8, 2048], P('dp', 'uly', 'blk'), may hold values from 7 to 9
- segments: int32 [2, 2048], P('dp'), may hold values from 0 to 15, never falling along the last dimension, each value on 1 to 256 neighbouring positions
- layer_input: bfloat16 [2, 2048, 4096], P('dp', ('blk', 'uly')), may hold values from -6 to 6
Outputs:
- query_grad: bfloat16 [2, 2048, 1024], P('dp', ('blk', 'uly'))
- keyvalue_grad: bfloat16 [2, 2048, 256], P('dp', ('blk', 'uly'))
- weight_grad: float32 [4096, 128], P(('uly', 'blk', 'dp'))
The draws below stay inside these ranges and needn't reach their ends.
Inputs may be any that keep to these rules, and one draw needn't show every extreme that they name: `segments`: document ids never fall along a sequence; each id covers 1 to 256 positions, and some id covers exactly that many.
All inputs are finite; a program needn't handle non-finite values.
Results may differ from the reference program's by a relative error of at most 0.0059.
Values may be sent and summed in bfloat16 or wider, within the bound.
A program may use at most 64 MiB of HBM per device.

```python
import math
import jax
import jax.numpy as jnp
import numpy as np
from jax import lax

HEAD_DIM = 128
GROUP_HEADS = 8
D_IN = 4096
BLOCK = 256
SEQ = 2048
SEQS = 2
TOKENS = 4096
N_BLK = 8


def raised(result, rng, source, target, blocks, factor):
    owner, partner = [(jnp.arange(result.shape[axis_at]) // (result.shape[axis_at] // blocks)).reshape([-1 if axis == axis_at else 1 for axis in range(result.ndim)]) for axis_at in (source, target)]
    chosen = jax.random.permutation(rng, blocks)[partner]
    strong = (owner == chosen) | (owner == (partner + blocks // 2) % blocks)
    return jnp.where(strong, factor * result, result)


def level_of(rng, dims, cuts, least, top_value):
    gain, own = 1.0, jax.random.fold_in(rng, 6)
    for axis_at, blocks in cuts:
        heights = jnp.exp(jax.random.uniform(jax.random.fold_in(own, axis_at), (blocks,), jnp.float32, least / len(cuts), top_value / len(cuts)))
        gain = gain * jnp.repeat(heights, dims[axis_at] // blocks).reshape([-1 if axis == axis_at else 1 for axis in range(len(dims))])
    return gain


def profile(number_of, total, most, slope):
    portions = [(1 << 20) // math.isqrt(rank ** slope) + 1 for rank in range(2, number_of + 1)]
    surplus, given = total - most - (number_of - 1), [1] * (number_of - 1)
    while surplus > 0:
        candidates = [i for i in range(number_of - 1) if given[i] < most]
        pool, remaining = sum([portions[i] for i in candidates]), surplus
        for i in candidates:
            more = min(most - given[i], max(1, remaining * portions[i] // pool), surplus)
            given[i] = given[i] + more
            surplus = surplus - more
    return np.array([most] + given)


def ragged(key, amount, total, bound, slope):
    if amount == 2:
        one = jax.random.randint(key, (), max(1, total - bound), min(bound, total - 1) + 1)
        return jnp.stack([one, total - one])
    sizes = jnp.asarray(profile(amount, total, bound, slope), jnp.int32)
    pairs = (amount - 1) // 2
    giver, sink = sizes[1:1 + 2 * pairs:2], sizes[2:2 + 2 * pairs:2]
    room = jnp.minimum(giver - 1, bound - sink)
    moved = jax.random.randint(jax.random.fold_in(key, 1), (pairs,), 0, 1 << 20) % (room + 1)
    sizes = sizes.at[1:1 + 2 * pairs:2].set(giver - moved).at[2:2 + 2 * pairs:2].set(sink + moved)
    return sizes[jax.random.permutation(jax.random.fold_in(key, 2), amount)]


def normal_values(own_key, dims, spread, most, pieces=(), kind=jnp.bfloat16):
    loudness = level_of(own_key, dims, pieces, -0.22, 0.18) if pieces else 1.0
    entries = jax.random.normal(own_key, dims, jnp.float32) * spread * loudness
    return jnp.minimum(jnp.maximum(entries, -most), most).astype(kind)


def gaussian_with(key, shape, width, limit, split, heavy, held_as=jnp.bfloat16):
    values = width * jax.random.normal(key, shape, jnp.float32)
    if split:
        values = values * level_of(key, shape, split, -0.22, 0.18)
    return jnp.clip(raised(values, jax.random.fold_in(key, 3), *heavy), -limit, limit).astype(held_as)


def setup_inputs(seed: int = 0) -> dict:
    arg_keys = jax.random.split(jax.random.key(seed), 8)
    queries = normal_values(arg_keys[0], (SEQS, SEQ, GROUP_HEADS * HEAD_DIM), 1.0, 6.0, ((0, 2), (1, 16)))
    out_grad = normal_values(arg_keys[1], (SEQS, SEQ, GROUP_HEADS * HEAD_DIM), 1.0, 6.0, ((0, 2), (1, 16)))
    keys_values = normal_values(arg_keys[2], (SEQS, SEQ, 2 * HEAD_DIM), 1.5, 9.0, ((0, 2), (1, 16)))
    attn_output = normal_values(arg_keys[3], (SEQS, GROUP_HEADS, SEQ, HEAD_DIM), 1.0, 6.0, ((0, 2), (1, 2), (2, 8)))
    logsumexp = jnp.clip(7.0 + 2.0 * jax.random.uniform(arg_keys[4], (SEQS, GROUP_HEADS, SEQ), jnp.float32) ** level_of(arg_keys[4], (SEQS, GROUP_HEADS, SEQ), ((0, 2), (1, 2), (2, 8)), -0.2, 0.2), 7.0, 9.0)
    segments = jax.vmap(lambda own: jnp.searchsorted(jnp.cumsum(ragged(own, 16, SEQ, SEQ // 8, 2)), jnp.arange(SEQ), side="right"))(jax.random.split(arg_keys[5], SEQS)).reshape((SEQS, SEQ)).astype(jnp.int32)
    layer_input = gaussian_with(arg_keys[6], (SEQS, SEQ, D_IN), 1.0, 6.0, ((0, 2), (1, 16)), (1, 2, 16, 2.0))
    return {"queries": queries, "out_grad": out_grad, "keys_values": keys_values, "attn_output": attn_output, "logsumexp": logsumexp, "segments": segments, "layer_input": layer_input}


def one_sequence(queries, out_grad, keys_values, attn_output, logsumexp, segments):
    scale = HEAD_DIM ** -0.5
    query_rows = queries.reshape(SEQ, GROUP_HEADS, HEAD_DIM)
    grad_rows = out_grad.reshape(SEQ, GROUP_HEADS, HEAD_DIM)
    delta = jnp.einsum('ihd,hid->hi', grad_rows.astype(jnp.float32), attn_output.astype(jnp.float32))
    padded_kv = jnp.concatenate([jnp.zeros((BLOCK, 2 * HEAD_DIM), keys_values.dtype), keys_values], axis=0)
    padded_seg = jnp.concatenate([jnp.full((BLOCK,), -1, jnp.int32), segments.astype(jnp.int32)], axis=0)

    def step(carry, block_index):
        start = (block_index * BLOCK).astype(jnp.int32)
        query_block = lax.dynamic_slice_in_dim(query_rows, start, BLOCK, 0).astype(jnp.float32)
        grad_block = lax.dynamic_slice_in_dim(grad_rows, start, BLOCK, 0).astype(jnp.float32)
        lse_block = lax.dynamic_slice_in_dim(logsumexp, start, BLOCK, 1)
        delta_block = lax.dynamic_slice_in_dim(delta, start, BLOCK, 1)
        window = lax.dynamic_slice_in_dim(padded_kv, start, 2 * BLOCK, 0).astype(jnp.float32)
        key_seg = lax.dynamic_slice_in_dim(padded_seg, start, 2 * BLOCK, 0)
        query_seg = lax.dynamic_slice_in_dim(segments.astype(jnp.int32), start, BLOCK, 0)
        query_pos = start + jnp.arange(BLOCK, dtype=jnp.int32)
        key_pos = start - BLOCK + jnp.arange(2 * BLOCK, dtype=jnp.int32)
        visible = (key_seg[None, :] == query_seg[:, None]) & (key_pos[None, :] <= query_pos[:, None]) & (key_pos[None, :] >= 0)
        keys_part = window[:, :HEAD_DIM]
        values_part = window[:, HEAD_DIM:]
        scores = jnp.einsum('qhd,kd->hqk', query_block, keys_part) * scale
        probs = jnp.where(visible[None], jnp.exp(scores - lse_block[:, :, None]), 0.0)
        dprobs = jnp.einsum('qhd,kd->hqk', grad_block, values_part)
        dscores = probs * (dprobs - delta_block[:, :, None])
        probs_low = lax.optimization_barrier(probs.astype(jnp.bfloat16)).astype(jnp.float32)
        dscores_low = lax.optimization_barrier(dscores.astype(jnp.bfloat16)).astype(jnp.float32)
        query_part = jnp.einsum('hqk,kd->qhd', dscores_low, keys_part) * scale
        key_part = jnp.einsum('hqk,qhd->kd', dscores_low, query_block) * scale
        value_part = jnp.einsum('hqk,qhd->kd', probs_low, grad_block)
        terms = jnp.concatenate([key_part, value_part], axis=1)
        finished = carry + terms[:BLOCK]
        return terms[BLOCK:], (query_part.reshape(BLOCK, GROUP_HEADS * HEAD_DIM).astype(jnp.bfloat16), finished)

    start_carry = jnp.zeros((BLOCK, 2 * HEAD_DIM), jnp.float32)
    last_block, (query_grad, finished) = lax.scan(step, start_carry, jnp.arange(N_BLK, dtype=jnp.int32))
    kv_grad = jnp.concatenate([finished[1:].reshape((N_BLK - 1) * BLOCK, 2 * HEAD_DIM), last_block], axis=0)
    return query_grad.reshape(SEQ, GROUP_HEADS * HEAD_DIM), kv_grad.astype(jnp.bfloat16)


def reference(queries, out_grad, keys_values, attn_output, logsumexp, segments, layer_input):
    query_list = []
    kv_list = []
    for seq_index in range(SEQS):
        query_grad, kv_grad = one_sequence(queries[seq_index], out_grad[seq_index], keys_values[seq_index], attn_output[seq_index], logsumexp[seq_index], segments[seq_index])
        query_list.append(query_grad)
        kv_list.append(kv_grad)
    query_all = jnp.stack(query_list)
    kv_all = jnp.stack(kv_list)
    flat_input = layer_input.reshape(TOKENS, D_IN)
    value_grads = kv_all.reshape(TOKENS, 2 * HEAD_DIM)[:, HEAD_DIM:]
    weight_grad = jnp.dot(flat_input.T, value_grads, preferred_element_type=jnp.float32) * (TOKENS ** -0.5)
    return (query_all, kv_all, weight_grad)
```

```python
import jax
import jax.numpy as jnp
from jax import lax
from jax.experimental import pallas as pl
from jax.experimental.pallas import tpu as pltpu
from jax.sharding import PartitionSpec as P

MESH = pl.DeviceIdType.MESH
HEAD = 128
HEADS = 8
CHUNK = 128
CHUNKS = 16
SLOTS = 3
GROUP = 16
HIDDEN = -1e30


def fused_kernel(
    q_hbm,
    g_hbm,
    kv_hbm,
    o_hbm,
    lse_hbm,
    seg_ref,
    x_hbm,
    dq_ref,
    dkv_ref,
    w_ref,
    qs,
    gs,
    kvb,
    ob,
    lb,
    p_all,
    ds_all,
    send_kv,
    recv_kv,
    xin,
    vg,
    part,
    part_in,
    q_sem,
    g_sem,
    own_sem,
    x_own_sem,
    kv_send,
    kv_recv,
    o_send,
    o_recv,
    ret_send,
    ret_recv,
    x_send,
    x_recv,
    v_send,
    v_recv,
    p_send,
    p_recv,
):
    rows, head_dim = CHUNK, HEAD
    uly = lax.axis_index("uly")
    blk = lax.axis_index("blk")
    dp = lax.axis_index("dp")
    chunk = blk * 2 + uly
    half = blk // 4
    member = uly * 8 + (blk % 4) * 2 + dp

    def at_chunk(index):
        index = lax.rem(index + CHUNKS, CHUNKS)
        return {"uly": index % 2, "blk": index // 2, "dp": dp}

    def at_member(index):
        index = lax.rem(index, GROUP)
        return {"uly": index // 8, "blk": half * 4 + (index % 8) // 2, "dp": index % 2}

    across = {"uly": 1 - uly, "blk": blk, "dp": dp}
    mirror = {"uly": uly, "blk": lax.rem(blk + 4, 8), "dp": dp}

    def cols_of(index, side):
        index = lax.rem(index, GROUP)
        return pl.ds(pl.multiple_of(((index // 8) * 16 + side * 8 + index % 8) * 128, 128), 128)

    loads = []
    for h in range(HEADS):
        at_rows, at_cols = pl.ds(h * rows, rows), pl.ds(h * head_dim, head_dim)
        loads.append(pltpu.make_async_copy(q_hbm.at[:, at_cols], qs.at[at_rows], q_sem.at[h]))
        loads.append(pltpu.make_async_copy(g_hbm.at[:, at_cols], gs.at[at_rows], g_sem.at[h]))
    mine = pl.ds(pl.multiple_of(uly * rows, rows), rows)
    theirs = pl.ds(pl.multiple_of((1 - uly) * rows, rows), rows)
    loads.append(pltpu.make_async_copy(kv_hbm, kvb.at[pl.ds(0, rows)], own_sem.at[0]))
    loads.append(pltpu.make_async_copy(o_hbm.at[:, mine], ob.at[uly], own_sem.at[1]))
    loads.append(pltpu.make_async_copy(lse_hbm.at[:, mine], lb.at[uly], own_sem.at[2]))
    for copy in loads:
        copy.start()
    x_own = [
        pltpu.make_async_copy(x_hbm.at[:, cols_of(member, side)], xin.at[side, 0], x_own_sem.at[side])
        for side in range(2)
    ]
    for copy in x_own:
        copy.start()

    barrier = pltpu.get_barrier_semaphore()
    for step in (1, 2, -1, -2):
        pl.semaphore_signal(barrier, inc=1, device_id=at_chunk(chunk + step), device_id_type=MESH)
    pl.semaphore_signal(barrier, inc=1, device_id=mirror, device_id_type=MESH)
    for k in range(1, GROUP):
        pl.semaphore_signal(barrier, inc=1, device_id=at_member(member + k), device_id_type=MESH)
    pl.semaphore_wait(barrier, GROUP - 1 + 5)

    def remote(src, dst, send, recv, device):
        return pltpu.make_async_remote_copy(
            src_ref=src,
            dst_ref=dst,
            send_sem=send,
            recv_sem=recv,
            device_id=device,
            device_id_type=MESH,
        )

    kv_out = [
        remote(
            kv_hbm, kvb.at[pl.ds(s * rows, rows)], kv_send.at[s - 1], kv_recv.at[s - 1], at_chunk(chunk + s)
        )
        for s in (1, 2)
    ]
    o_out = [
        remote(o_hbm.at[:, theirs], ob.at[uly], o_send.at[0], o_recv.at[0], across),
        remote(lse_hbm.at[:, theirs], lb.at[uly], o_send.at[1], o_recv.at[1], across),
    ]
    for copy in kv_out + o_out:
        copy.start()
    x_out = [
        remote(
            x_hbm.at[:, cols_of(member + k, side)],
            xin.at[side, k],
            x_send.at[side, k],
            x_recv.at[side, k],
            at_member(member + k),
        )
        for k in range(1, GROUP)
        for side in range(2)
    ]
    for copy in x_out:
        copy.start()

    lane_query = lax.broadcasted_iota(jnp.int32, (rows, rows), 1)
    row_key = lax.broadcasted_iota(jnp.int32, (rows, rows), 0)

    def seg_row(index):
        index = lax.rem(index + CHUNKS, CHUNKS)
        return seg_ref[:, pl.ds(pl.multiple_of(index * rows, rows), rows)]

    own_seg = jnp.broadcast_to(seg_row(chunk), (rows, rows))
    biases = []
    for s in range(SLOTS):
        key_seg = jnp.broadcast_to(seg_row(chunk - s), (rows, rows)).T
        seen = (key_seg == own_seg) & (chunk >= s)
        if s == 0:
            seen = seen & (row_key <= lane_query)
        biases.append(jnp.where(seen, 0.0, HIDDEN))
    bias = jnp.concatenate(biases, axis=0)
    bias = jnp.concatenate([bias, bias], axis=1)

    for copy in loads:
        copy.wait()
    for copy in o_out + kv_out:
        copy.wait_recv()
    scale = head_dim ** (-0.5)
    across_dims = (((1,), (1,)), ((), ()))
    keys = kvb[:, :head_dim]
    values = kvb[:, head_dim:]
    for pair in range(HEADS // 2):
        at_rows = slice(pair * 2 * rows, (pair + 1) * 2 * rows)
        q_pair = qs[at_rows, :]
        g_pair = gs[at_rows, :]
        deltas, lses = [], []
        for h in (2 * pair, 2 * pair + 1):
            prods = lax.dot_general(
                ob[h // 4, h % 4],
                gs[h * rows : (h + 1) * rows, :],
                across_dims,
                preferred_element_type=jnp.float32,
            )
            deltas.append(
                jnp.sum(jnp.where(row_key == lane_query, prods, 0.0), axis=0, keepdims=True)
            )
            lses.append(lb[h // 4, h % 4 : h % 4 + 1, :])
        delta = jnp.concatenate(deltas, axis=1)
        lse = jnp.concatenate(lses, axis=1)
        scores = lax.dot_general(keys, q_pair, across_dims, preferred_element_type=jnp.float32)
        dprob = lax.dot_general(values, g_pair, across_dims, preferred_element_type=jnp.float32)
        prob = jnp.exp(scores * scale - lse + bias)
        p_all[:, at_rows] = prob.astype(jnp.bfloat16)
        ds_all[:, at_rows] = (prob * (dprob - delta)).astype(jnp.bfloat16)

    dk = jnp.dot(ds_all[rows:, :], qs[...], preferred_element_type=jnp.float32) * scale
    send_kv[:, :, :head_dim] = dk.reshape(2, rows, head_dim)
    dv = jnp.dot(p_all[rows:, :], gs[...], preferred_element_type=jnp.float32)
    send_kv[:, :, head_dim:] = dv.reshape(2, rows, head_dim)
    returns = [
        remote(send_kv.at[s - 1], recv_kv.at[s - 1], ret_send.at[s - 1], ret_recv.at[s - 1], at_chunk(chunk - s))
        for s in (1, 2)
    ]
    for copy in returns:
        copy.start()
    dv_own = jnp.dot(p_all[:rows, :], gs[...], preferred_element_type=jnp.float32)
    dk_own = jnp.dot(ds_all[:rows, :], qs[...], preferred_element_type=jnp.float32) * scale
    for h in range(HEADS):
        at_rows = slice(h * rows, (h + 1) * rows)
        dq = lax.dot_general(
            ds_all[:, at_rows], keys, (((0,), (0,)), ((), ())), preferred_element_type=jnp.float32
        )
        dq_ref[:, at_rows] = (dq * scale).astype(jnp.bfloat16)

    for copy in returns:
        copy.wait_recv()
    value_grad = (dv_own + recv_kv[0, :, head_dim:] + recv_kv[1, :, head_dim:]).astype(jnp.bfloat16)
    vg[0] = value_grad
    v_out = [
        remote(vg.at[0], vg.at[k], v_send.at[k], v_recv.at[k], at_member(member + k))
        for k in range(1, GROUP)
    ]
    for copy in v_out:
        copy.start()
    dkv_ref[:, head_dim:] = value_grad
    dkv_ref[:, :head_dim] = (dk_own + recv_kv[0, :, :head_dim] + recv_kv[1, :, :head_dim]).astype(
        jnp.bfloat16
    )

    for copy in x_own:
        copy.wait()
    for copy in x_out:
        copy.wait_recv()
    for copy in v_out:
        copy.wait_recv()
    grads = vg[...].reshape(GROUP * rows, head_dim)
    for side in range(2):
        part[side] = lax.dot_general(
            xin[side].reshape(GROUP * rows, 128),
            grads,
            (((0,), (0,)), ((), ())),
            preferred_element_type=jnp.float32,
        )
    swap = remote(part.at[1 - half], part_in, p_send.at[0], p_recv.at[0], mirror)
    swap.start()
    swap.wait_recv()
    w_ref[...] = (part[half] + part_in[...]) * (rows * CHUNKS * 2) ** (-0.5)
    for copy in kv_out + o_out + x_out + returns + v_out + [swap]:
        copy.wait_send()


def fused(queries, out_grad, keys_values, attn_output, logsumexp, segments, layer_input):
    anywhere = pl.BlockSpec(memory_space=pl.ANY)
    in_vmem = pl.BlockSpec(memory_space=pltpu.VMEM)
    low, full = jnp.bfloat16, jnp.float32
    dma = pltpu.SemaphoreType.DMA
    width = HEADS * HEAD
    dq, dkv, weight = pl.pallas_call(
        fused_kernel,
        out_shape=(
            jax.ShapeDtypeStruct((CHUNK, width), low),
            jax.ShapeDtypeStruct((CHUNK, 2 * HEAD), low),
            jax.ShapeDtypeStruct((128, HEAD), full),
        ),
        in_specs=[anywhere] * 5 + [in_vmem, anywhere],
        out_specs=(in_vmem, in_vmem, in_vmem),
        scratch_shapes=[
            pltpu.VMEM((width, HEAD), low),
            pltpu.VMEM((width, HEAD), low),
            pltpu.VMEM((SLOTS * CHUNK, 2 * HEAD), low),
            pltpu.VMEM((2, HEADS // 2, CHUNK, HEAD), low),
            pltpu.VMEM((2, HEADS // 2, CHUNK), full),
            pltpu.VMEM((SLOTS * CHUNK, width), low),
            pltpu.VMEM((SLOTS * CHUNK, width), low),
            pltpu.VMEM((2, CHUNK, 2 * HEAD), full),
            pltpu.VMEM((2, CHUNK, 2 * HEAD), full),
            pltpu.VMEM((2, GROUP, CHUNK, 128), low),
            pltpu.VMEM((GROUP, CHUNK, HEAD), low),
            pltpu.VMEM((2, 128, HEAD), full),
            pltpu.VMEM((128, HEAD), full),
            dma((HEADS,)),
            dma((HEADS,)),
            dma((3,)),
            dma((2,)),
            dma((2,)),
            dma((2,)),
            dma((2,)),
            dma((2,)),
            dma((2,)),
            dma((2,)),
            dma((2, GROUP)),
            dma((2, GROUP)),
            dma((GROUP,)),
            dma((GROUP,)),
            dma((1,)),
            dma((1,)),
        ],
        compiler_params=pltpu.CompilerParams(
            collective_id=0, has_side_effects=True, vmem_limit_bytes=32 * 1024 * 1024
        ),
    )(
        queries[0],
        out_grad[0],
        keys_values[0],
        attn_output[0],
        logsumexp[0],
        segments,
        layer_input[0],
    )
    return dq[None], dkv[None], weight


def passed_along(shard, axis, by):
    devices = lax.axis_size(axis)
    pairs = [(i, i + by) for i in range(devices) if 0 <= i + by < devices]
    return lax.ppermute(shard, axis, pairs)


def block_grads(
    query_rows, grad_rows, lse_rows, delta_rows, query_start, key_block, key_start, seq_ids, live
):
    block_rows = query_rows.shape[0]
    local_heads = lse_rows.shape[0]
    head_dim = key_block.shape[1] // 2
    key_rows = key_block.shape[0]
    seq_len = seq_ids.shape[0]
    tile_rows = min(512, block_rows)
    tile_count = block_rows // tile_rows
    scale = head_dim ** (-0.5)
    query_tiles = query_rows.reshape(tile_count, tile_rows, local_heads, head_dim)
    grad_tiles = grad_rows.reshape(tile_count, tile_rows, local_heads, head_dim)
    lse_tiles = lse_rows.reshape(local_heads, tile_count, tile_rows).transpose(1, 0, 2)
    delta_tiles = delta_rows.reshape(local_heads, tile_count, tile_rows).transpose(1, 0, 2)
    keys_part = key_block[:, :head_dim]
    values_part = key_block[:, head_dim:]
    key_pos = key_start + jnp.arange(key_rows, dtype=jnp.int32)
    key_seg = lax.dynamic_slice_in_dim(
        seq_ids, jnp.clip(key_start, 0, seq_len - key_rows), key_rows, 0
    )

    def tile_step(carry, pieces):
        tile_index, query_tile, grad_tile, lse_tile, delta_tile = pieces
        tile_start = query_start + tile_index * tile_rows
        query_pos = tile_start + jnp.arange(tile_rows, dtype=jnp.int32)
        query_seg = lax.dynamic_slice_in_dim(
            seq_ids, jnp.clip(tile_start, 0, seq_len - tile_rows), tile_rows, 0
        )
        visible = (
            live
            & (key_seg[None, :] == query_seg[:, None])
            & (key_pos[None, :] <= query_pos[:, None])
        )
        scores = (
            jnp.einsum("qhd,kd->hqk", query_tile, keys_part, preferred_element_type=jnp.float32)
            * scale
        )
        probs = jnp.where(visible[None], jnp.exp(scores - lse_tile[:, :, None]), 0.0)
        dprobs = jnp.einsum(
            "qhd,kd->hqk", grad_tile, values_part, preferred_element_type=jnp.float32
        )
        dscores = probs * (dprobs - delta_tile[:, :, None])
        probs_low = probs.astype(jnp.bfloat16)
        dscores_low = dscores.astype(jnp.bfloat16)
        query_part = (
            jnp.einsum("hqk,kd->qhd", dscores_low, keys_part, preferred_element_type=jnp.float32)
            * scale
        )
        key_part = (
            jnp.einsum("hqk,qhd->kd", dscores_low, query_tile, preferred_element_type=jnp.float32)
            * scale
        )
        value_part = jnp.einsum(
            "hqk,qhd->kd", probs_low, grad_tile, preferred_element_type=jnp.float32
        )
        query_part, kv_part = (query_part, jnp.concatenate([key_part, value_part], axis=1))
        return (carry + kv_part, query_part)

    start_total = jnp.zeros((key_rows, 2 * head_dim), jnp.float32)
    kv_total, query_parts = lax.scan(
        tile_step,
        start_total,
        (jnp.arange(tile_count, dtype=jnp.int32), query_tiles, grad_tiles, lse_tiles, delta_tiles),
    )
    return (query_parts.reshape(block_rows, local_heads * head_dim), kv_total)


def on_device(queries, out_grad, keys_values, attn_output, logsumexp, segments, layer_input):
    head_dim = keys_values.shape[2] // 2
    query_heads, grad_heads = (
        lax.all_to_all(queries, "uly", split_axis=2, concat_axis=1, tiled=True),
        lax.all_to_all(out_grad, "uly", split_axis=2, concat_axis=1, tiled=True),
    )
    key_block = lax.all_gather(keys_values, "uly", axis=1, tiled=True)[0]
    query_rows = query_heads[0]
    grad_rows = grad_heads[0]
    block_rows = query_rows.shape[0]
    local_heads = attn_output.shape[1]
    lse_rows = logsumexp[0]
    delta_rows = jnp.einsum(
        "thd,htd->ht",
        grad_rows.reshape(block_rows, local_heads, head_dim),
        attn_output[0],
        preferred_element_type=jnp.float32,
    )
    seq_ids = segments[0]
    cycle_index = lax.axis_index("blk")
    own_start = cycle_index * block_rows
    always_live = jnp.asarray(True)
    query_own, kv_own = block_grads(
        query_rows,
        grad_rows,
        lse_rows,
        delta_rows,
        own_start,
        key_block,
        own_start,
        seq_ids,
        always_live,
    )
    key_before = passed_along(key_block, "blk", 1)
    query_before, kv_before = block_grads(
        query_rows,
        grad_rows,
        lse_rows,
        delta_rows,
        own_start,
        key_before,
        own_start - block_rows,
        seq_ids,
        cycle_index >= 1,
    )
    kv_returned = passed_along(kv_before, "blk", -1)
    query_total = query_own + query_before
    kv_total = kv_own + kv_returned
    kv_sums = lax.psum_scatter(kv_total, "uly", scatter_dimension=0, tiled=True)
    kv_grad = kv_sums.astype(jnp.bfloat16)
    query_grad = lax.all_to_all(
        query_total.astype(jnp.bfloat16)[None], "uly", split_axis=1, concat_axis=2, tiled=True
    )
    value_grads = kv_grad[:, head_dim:]
    all_devices = lax.axis_size(("uly", "blk", "dp"))
    total_tokens = layer_input.shape[1] * all_devices
    flat_input = layer_input[0]
    weight_sum = lax.psum_scatter(
        lax.dot_general(
            flat_input, value_grads, (((0,), (0,)), ((), ())), preferred_element_type=jnp.float32
        ),
        ("uly", "blk", "dp"),
        scatter_dimension=0,
        tiled=True,
    )
    return (query_grad, kv_grad[None], weight_sum * total_tokens ** (-0.5))


def solution(mesh):
    placed = (
        P("dp", ("blk", "uly"), None),
        P("dp", ("blk", "uly"), None),
        P("dp", ("blk", "uly"), None),
        P("dp", "uly", "blk", None),
        P("dp", "uly", "blk"),
        P("dp", None),
        P("dp", ("blk", "uly"), None),
    )
    small = tuple(mesh.shape[axis] for axis in ("uly", "blk", "dp")) == (2, 8, 2)
    return jax.shard_map(
        fused if small else on_device,
        mesh=mesh,
        in_specs=placed,
        out_specs=(
            P("dp", ("blk", "uly"), None),
            P("dp", ("blk", "uly"), None),
            P(("uly", "blk", "dp"), None),
        ),
        check_vma=False,
    )
```

```python
import jax
import jax.numpy as jnp
from jax import lax
from jax.experimental import pallas as pl
from jax.experimental.pallas import tpu as pltpu
from jax.sharding import PartitionSpec as P

MESH = pl.DeviceIdType.MESH
HEAD = 128
HEADS = 8
CHUNK = 128
CHUNKS = 16
SLOTS = 3
GROUP = 8
CORNERS = 4
HIDDEN = -1e30
LOG2E = 1.4426950408889634


def fused_kernel(
    q_hbm,
    g_hbm,
    kv_hbm,
    o_hbm,
    lse_hbm,
    seg_ref,
    x_hbm,
    dq_ref,
    dkv_ref,
    w_ref,
    qs,
    gs,
    kb,
    vb,
    ob,
    lb,
    p_full,
    p_all,
    ds_all,
    send_kv,
    recv_kv,
    xin,
    vg,
    part,
    part_low,
    part_in,
    q_sem,
    g_sem,
    own_sem,
    x_own_sem,
    kv_send,
    kv_recv,
    o_send,
    o_recv,
    ret_send,
    ret_recv,
    x_send,
    x_recv,
    v_send,
    v_recv,
    p_send,
    p_recv,
):
    rows, head_dim = CHUNK, HEAD
    low, full = jnp.bfloat16, jnp.float32
    uly = lax.axis_index("uly")
    blk = lax.axis_index("blk")
    dp = lax.axis_index("dp")
    chunk = blk * 2 + uly
    half = blk // 4
    member = (blk % 4) * 2 + dp
    corner = uly * 2 + half

    def at_chunk(index):
        index = lax.rem(index + CHUNKS, CHUNKS)
        return {"uly": index % 2, "blk": index // 2, "dp": dp}

    def at_member(index):
        index = lax.rem(index, GROUP)
        return {"uly": uly, "blk": half * 4 + index // 2, "dp": index % 2}

    def at_corner(index):
        index = lax.rem(index, CORNERS)
        return {"uly": index // 2, "blk": (index % 2) * 4 + blk % 4, "dp": dp}

    across = {"uly": 1 - uly, "blk": blk, "dp": dp}

    def cols_of(index, side):
        index = lax.rem(index, GROUP)
        first = (side // 2) * 16 + (side % 2) * 8
        return pl.ds(pl.multiple_of((first + index) * 128, 128), 128)

    def lanes(side):
        return pl.ds(side * 128, 128)

    loads = []
    for h in range(HEADS):
        at_rows, at_cols = pl.ds(h * rows, rows), pl.ds(h * head_dim, head_dim)
        loads.append(pltpu.make_async_copy(q_hbm.at[:, at_cols], qs.at[at_rows], q_sem.at[h]))
        loads.append(pltpu.make_async_copy(g_hbm.at[:, at_cols], gs.at[at_rows], g_sem.at[h]))
    mine = pl.ds(pl.multiple_of(uly * rows, rows), rows)
    theirs = pl.ds(pl.multiple_of((1 - uly) * rows, rows), rows)
    own = pl.ds(0, rows)
    keys_at, values_at = pl.ds(0, head_dim), pl.ds(head_dim, head_dim)
    loads.append(pltpu.make_async_copy(kv_hbm.at[:, keys_at], kb.at[own], own_sem.at[0]))
    loads.append(pltpu.make_async_copy(kv_hbm.at[:, values_at], vb.at[own], own_sem.at[1]))
    loads.append(pltpu.make_async_copy(o_hbm.at[:, mine], ob.at[uly], own_sem.at[2]))
    loads.append(pltpu.make_async_copy(lse_hbm.at[:, mine], lb.at[uly], own_sem.at[3]))
    x_own = [
        pltpu.make_async_copy(
            x_hbm.at[:, cols_of(member, side)], xin.at[0, :, lanes(side)], x_own_sem.at[side]
        )
        for side in range(CORNERS)
    ]

    barrier = pltpu.get_barrier_semaphore()
    for step in (1, 2, -1, -2):
        pl.semaphore_signal(barrier, inc=1, device_id=at_chunk(chunk + step), device_id_type=MESH)
    for k in range(1, CORNERS):
        pl.semaphore_signal(barrier, inc=1, device_id=at_corner(corner + k), device_id_type=MESH)
    for k in range(1, GROUP):
        pl.semaphore_signal(barrier, inc=1, device_id=at_member(member + k), device_id_type=MESH)
    for copy in loads + x_own:
        copy.start()

    lane_query = lax.broadcasted_iota(jnp.int32, (rows, rows), 1)
    row_key = lax.broadcasted_iota(jnp.int32, (rows, rows), 0)

    def seg_row(index):
        index = lax.rem(index + CHUNKS, CHUNKS)
        return seg_ref[:, pl.ds(pl.multiple_of(index * rows, rows), rows)]

    own_seg = jnp.broadcast_to(seg_row(chunk), (rows, rows))
    biases = []
    for s in range(SLOTS):
        key_seg = jnp.broadcast_to(seg_row(chunk - s), (rows, rows)).T
        seen = (key_seg == own_seg) & (chunk >= s)
        if s == 0:
            seen = seen & (row_key <= lane_query)
        biases.append(jnp.where(seen, 0.0, HIDDEN))
    bias = jnp.concatenate(biases, axis=0)
    bias = jnp.concatenate([bias, bias], axis=1)

    pl.semaphore_wait(barrier, GROUP - 1 + CORNERS - 1 + 4)

    def remote(src, dst, send, recv, device):
        return pltpu.make_async_remote_copy(
            src_ref=src,
            dst_ref=dst,
            send_sem=send,
            recv_sem=recv,
            device_id=device,
            device_id_type=MESH,
        )

    def to_chunks(columns, buffer, first):
        return [
            remote(
                kv_hbm.at[:, columns],
                buffer.at[pl.ds(s * rows, rows)],
                kv_send.at[first + s - 1],
                kv_recv.at[first + s - 1],
                at_chunk(chunk + s),
            )
            for s in (1, 2)
        ]

    keys_out = to_chunks(keys_at, kb, 0)
    lse_out = remote(lse_hbm.at[:, theirs], lb.at[uly], o_send.at[1], o_recv.at[1], across)
    values_out = to_chunks(values_at, vb, 2)
    o_out = remote(o_hbm.at[:, theirs], ob.at[uly], o_send.at[0], o_recv.at[0], across)
    early, later = keys_out + [lse_out], values_out + [o_out]
    for copy in early + later:
        copy.start()
    x_out = [
        remote(
            x_hbm.at[:, cols_of(member + k, side)],
            xin.at[k, :, lanes(side)],
            x_send.at[side, k],
            x_recv.at[side, k],
            at_member(member + k),
        )
        for k in range(1, GROUP)
        for side in range(CORNERS)
    ]
    for copy in x_out:
        copy.start()

    for copy in loads:
        copy.wait()
    for copy in early:
        copy.wait_recv()
    scale = head_dim ** (-0.5)
    across_dims = (((1,), (1,)), ((), ()))
    pairs = [slice(pair * 2 * rows, (pair + 1) * 2 * rows) for pair in range(HEADS // 2)]

    def probs_of(part_rows):
        for pair, at_rows in enumerate(pairs):
            lse = jnp.concatenate(
                [lb[h // 4, h % 4 : h % 4 + 1, :] for h in (2 * pair, 2 * pair + 1)], axis=1
            )
            scores = lax.dot_general(
                kb[part_rows, :], qs[at_rows, :], across_dims, preferred_element_type=full
            )
            prob = jnp.exp2(scores * (scale * LOG2E) - lse * LOG2E + bias[part_rows])
            p_full[part_rows, at_rows] = prob
            p_all[part_rows, at_rows] = prob.astype(low)

    def returned(index):
        return [
            remote(
                send_kv.at[index, s - 1],
                recv_kv.at[index, s - 1],
                ret_send.at[index, s - 1],
                ret_recv.at[index, s - 1],
                at_chunk(chunk - s),
            )
            for s in (1, 2)
        ]

    before, here = slice(rows, SLOTS * rows), slice(0, rows)
    probs_of(before)
    dv = jnp.dot(p_all[before, :], gs[...], preferred_element_type=full)
    send_kv[0] = dv.astype(low).reshape(2, rows, head_dim)
    dv_back = returned(0)
    for copy in dv_back:
        copy.start()
    probs_of(here)
    dv_own = jnp.dot(p_all[here, :], gs[...], preferred_element_type=full)

    for copy in dv_back:
        copy.wait_recv()
    value_grad = dv_own + recv_kv[0, 0].astype(full) + recv_kv[0, 1].astype(full)
    vg[0] = value_grad.T.astype(low)
    v_out = [
        remote(vg.at[0], vg.at[k], v_send.at[k], v_recv.at[k], at_member(member + k))
        for k in range(1, GROUP)
    ]
    for copy in v_out:
        copy.start()
    dkv_ref[:, head_dim:] = value_grad.astype(low)

    for copy in later:
        copy.wait_recv()
    for pair, at_rows in enumerate(pairs):
        deltas = []
        for h in (2 * pair, 2 * pair + 1):
            prods = lax.dot_general(
                ob[h // 4, h % 4],
                gs[h * rows : (h + 1) * rows, :],
                across_dims,
                preferred_element_type=full,
            )
            deltas.append(
                jnp.sum(jnp.where(row_key == lane_query, prods, 0.0), axis=0, keepdims=True)
            )
        delta = jnp.concatenate(deltas, axis=1)
        dprob = lax.dot_general(vb[...], gs[at_rows, :], across_dims, preferred_element_type=full)
        ds_all[:, at_rows] = (p_full[:, at_rows] * (dprob - delta)).astype(low)
    dk = jnp.dot(ds_all[before, :], qs[...], preferred_element_type=full) * scale
    send_kv[1] = dk.astype(low).reshape(2, rows, head_dim)
    dk_back = returned(1)
    for copy in dk_back:
        copy.start()

    for copy in x_own:
        copy.wait()
    total = None
    for first in range(0, GROUP, 2):
        for k in (first, first + 1):
            if k > 0:
                v_out[k - 1].wait_recv()
                for side in range(CORNERS):
                    x_out[(k - 1) * CORNERS + side].wait_recv()
        term = jnp.dot(
            jnp.concatenate([vg[first], vg[first + 1]], axis=1),
            xin[first : first + 2].reshape(2 * rows, CORNERS * 128),
            preferred_element_type=full,
        )
        total = term if total is None else total + term
    for side in range(CORNERS):
        piece = total[:, side * 128 : (side + 1) * 128]
        part[side] = piece
        part_low[side] = piece.astype(low)
    sums = [
        remote(
            part_low.at[lax.rem(corner + k, CORNERS)],
            part_in.at[k],
            p_send.at[k],
            p_recv.at[k],
            at_corner(corner + k),
        )
        for k in range(1, CORNERS)
    ]
    for copy in sums:
        copy.start()

    dk_own = jnp.dot(ds_all[here, :], qs[...], preferred_element_type=full) * scale
    for h in range(HEADS):
        at_rows = slice(h * rows, (h + 1) * rows)
        dq = lax.dot_general(
            ds_all[:, at_rows], kb[...], (((0,), (0,)), ((), ())), preferred_element_type=full
        )
        dq_ref[:, at_rows] = (dq * scale).astype(low)
    for copy in dk_back:
        copy.wait_recv()
    dkv_ref[:, :head_dim] = (
        dk_own + recv_kv[1, 0].astype(full) + recv_kv[1, 1].astype(full)
    ).astype(low)
    weight = part[corner]
    for k, copy in enumerate(sums, 1):
        copy.wait_recv()
        weight = weight + part_in[k].astype(full)
    w_ref[...] = weight.T * (rows * CHUNKS * 2) ** (-0.5)
    for copy in early + later + x_out + dv_back + dk_back + v_out + sums:
        copy.wait_send()


def written(*refs):
    half = len(refs) // 2
    sources, results, sems = refs[:half], refs[half : 2 * half], refs[-1]
    copies = [
        pltpu.make_async_copy(source, result, sems.at[i])
        for i, (source, result) in enumerate(zip(sources, results))
    ]
    for copy in copies:
        copy.start()
    for copy in copies:
        copy.wait()


def fused(queries, out_grad, keys_values, attn_output, logsumexp, segments, layer_input):
    anywhere = pl.BlockSpec(memory_space=pl.ANY)
    in_vmem = pl.BlockSpec(memory_space=pltpu.VMEM)
    low, full = jnp.bfloat16, jnp.float32
    dma = pltpu.SemaphoreType.DMA
    width = HEADS * HEAD
    results = (
        jax.ShapeDtypeStruct((CHUNK, width), low),
        jax.ShapeDtypeStruct((CHUNK, 2 * HEAD), low),
        jax.ShapeDtypeStruct((128, HEAD), full),
    )
    found = pl.pallas_call(
        fused_kernel,
        out_shape=results,
        in_specs=[anywhere] * 5 + [in_vmem, anywhere],
        out_specs=(in_vmem, in_vmem, in_vmem),
        scratch_shapes=[
            pltpu.VMEM((width, HEAD), low),
            pltpu.VMEM((width, HEAD), low),
            pltpu.VMEM((SLOTS * CHUNK, HEAD), low),
            pltpu.VMEM((SLOTS * CHUNK, HEAD), low),
            pltpu.VMEM((2, HEADS // 2, CHUNK, HEAD), low),
            pltpu.VMEM((2, HEADS // 2, CHUNK), full),
            pltpu.VMEM((SLOTS * CHUNK, width), full),
            pltpu.VMEM((SLOTS * CHUNK, width), low),
            pltpu.VMEM((SLOTS * CHUNK, width), low),
            pltpu.VMEM((2, 2, CHUNK, HEAD), low),
            pltpu.VMEM((2, 2, CHUNK, HEAD), low),
            pltpu.VMEM((GROUP, CHUNK, CORNERS * 128), low),
            pltpu.VMEM((GROUP, HEAD, CHUNK), low),
            pltpu.VMEM((CORNERS, HEAD, 128), full),
            pltpu.VMEM((CORNERS, HEAD, 128), low),
            pltpu.VMEM((CORNERS, HEAD, 128), low),
            dma((HEADS,)),
            dma((HEADS,)),
            dma((4,)),
            dma((CORNERS,)),
            dma((4,)),
            dma((4,)),
            dma((2,)),
            dma((2,)),
            dma((2, 2)),
            dma((2, 2)),
            dma((CORNERS, GROUP)),
            dma((CORNERS, GROUP)),
            dma((GROUP,)),
            dma((GROUP,)),
            dma((CORNERS,)),
            dma((CORNERS,)),
        ],
        compiler_params=pltpu.CompilerParams(
            collective_id=0, has_side_effects=True, vmem_limit_bytes=60 * 1024 * 1024
        ),
    )(
        queries[0],
        out_grad[0],
        keys_values[0],
        attn_output[0],
        logsumexp[0],
        segments,
        layer_input[0],
    )
    dq, dkv, weight = pl.pallas_call(
        written,
        out_shape=results,
        in_specs=[anywhere] * 3,
        out_specs=(anywhere,) * 3,
        scratch_shapes=[dma((3,))],
    )(*found)
    return dq[None], dkv[None], weight


def passed_along(shard, axis, by):
    devices = lax.axis_size(axis)
    pairs = [(i, i + by) for i in range(devices) if 0 <= i + by < devices]
    return lax.ppermute(shard, axis, pairs)


def block_grads(
    query_rows, grad_rows, lse_rows, delta_rows, query_start, key_block, key_start, seq_ids, live
):
    block_rows = query_rows.shape[0]
    local_heads = lse_rows.shape[0]
    head_dim = key_block.shape[1] // 2
    key_rows = key_block.shape[0]
    seq_len = seq_ids.shape[0]
    tile_rows = min(512, block_rows)
    tile_count = block_rows // tile_rows
    scale = head_dim ** (-0.5)
    query_tiles = query_rows.reshape(tile_count, tile_rows, local_heads, head_dim)
    grad_tiles = grad_rows.reshape(tile_count, tile_rows, local_heads, head_dim)
    lse_tiles = lse_rows.reshape(local_heads, tile_count, tile_rows).transpose(1, 0, 2)
    delta_tiles = delta_rows.reshape(local_heads, tile_count, tile_rows).transpose(1, 0, 2)
    keys_part = key_block[:, :head_dim]
    values_part = key_block[:, head_dim:]
    key_pos = key_start + jnp.arange(key_rows, dtype=jnp.int32)
    key_seg = lax.dynamic_slice_in_dim(
        seq_ids, jnp.clip(key_start, 0, seq_len - key_rows), key_rows, 0
    )

    def tile_step(carry, pieces):
        tile_index, query_tile, grad_tile, lse_tile, delta_tile = pieces
        tile_start = query_start + tile_index * tile_rows
        query_pos = tile_start + jnp.arange(tile_rows, dtype=jnp.int32)
        query_seg = lax.dynamic_slice_in_dim(
            seq_ids, jnp.clip(tile_start, 0, seq_len - tile_rows), tile_rows, 0
        )
        visible = (
            live
            & (key_seg[None, :] == query_seg[:, None])
            & (key_pos[None, :] <= query_pos[:, None])
        )
        scores = (
            jnp.einsum("qhd,kd->hqk", query_tile, keys_part, preferred_element_type=jnp.float32)
            * scale
        )
        probs = jnp.where(visible[None], jnp.exp(scores - lse_tile[:, :, None]), 0.0)
        dprobs = jnp.einsum(
            "qhd,kd->hqk", grad_tile, values_part, preferred_element_type=jnp.float32
        )
        dscores = probs * (dprobs - delta_tile[:, :, None])
        probs_low = probs.astype(jnp.bfloat16)
        dscores_low = dscores.astype(jnp.bfloat16)
        query_part = (
            jnp.einsum("hqk,kd->qhd", dscores_low, keys_part, preferred_element_type=jnp.float32)
            * scale
        )
        key_part = (
            jnp.einsum("hqk,qhd->kd", dscores_low, query_tile, preferred_element_type=jnp.float32)
            * scale
        )
        value_part = jnp.einsum(
            "hqk,qhd->kd", probs_low, grad_tile, preferred_element_type=jnp.float32
        )
        query_part, kv_part = (query_part, jnp.concatenate([key_part, value_part], axis=1))
        return (carry + kv_part, query_part)

    start_total = jnp.zeros((key_rows, 2 * head_dim), jnp.float32)
    kv_total, query_parts = lax.scan(
        tile_step,
        start_total,
        (jnp.arange(tile_count, dtype=jnp.int32), query_tiles, grad_tiles, lse_tiles, delta_tiles),
    )
    return (query_parts.reshape(block_rows, local_heads * head_dim), kv_total)


def on_device(queries, out_grad, keys_values, attn_output, logsumexp, segments, layer_input):
    head_dim = keys_values.shape[2] // 2
    query_heads, grad_heads = (
        lax.all_to_all(queries, "uly", split_axis=2, concat_axis=1, tiled=True),
        lax.all_to_all(out_grad, "uly", split_axis=2, concat_axis=1, tiled=True),
    )
    key_block = lax.all_gather(keys_values, "uly", axis=1, tiled=True)[0]
    query_rows = query_heads[0]
    grad_rows = grad_heads[0]
    block_rows = query_rows.shape[0]
    local_heads = attn_output.shape[1]
    lse_rows = logsumexp[0]
    delta_rows = jnp.einsum(
        "thd,htd->ht",
        grad_rows.reshape(block_rows, local_heads, head_dim),
        attn_output[0],
        preferred_element_type=jnp.float32,
    )
    seq_ids = segments[0]
    cycle_index = lax.axis_index("blk")
    own_start = cycle_index * block_rows
    always_live = jnp.asarray(True)
    query_own, kv_own = block_grads(
        query_rows,
        grad_rows,
        lse_rows,
        delta_rows,
        own_start,
        key_block,
        own_start,
        seq_ids,
        always_live,
    )
    key_before = passed_along(key_block, "blk", 1)
    query_before, kv_before = block_grads(
        query_rows,
        grad_rows,
        lse_rows,
        delta_rows,
        own_start,
        key_before,
        own_start - block_rows,
        seq_ids,
        cycle_index >= 1,
    )
    kv_returned = passed_along(kv_before, "blk", -1)
    query_total = query_own + query_before
    kv_total = kv_own + kv_returned
    kv_sums = lax.psum_scatter(kv_total, "uly", scatter_dimension=0, tiled=True)
    kv_grad = kv_sums.astype(jnp.bfloat16)
    query_grad = lax.all_to_all(
        query_total.astype(jnp.bfloat16)[None], "uly", split_axis=1, concat_axis=2, tiled=True
    )
    value_grads = kv_grad[:, head_dim:]
    all_devices = lax.axis_size(("uly", "blk", "dp"))
    total_tokens = layer_input.shape[1] * all_devices
    flat_input = layer_input[0]
    weight_sum = lax.psum_scatter(
        lax.dot_general(
            flat_input, value_grads, (((0,), (0,)), ((), ())), preferred_element_type=jnp.float32
        ),
        ("uly", "blk", "dp"),
        scatter_dimension=0,
        tiled=True,
    )
    return (query_grad, kv_grad[None], weight_sum * total_tokens ** (-0.5))


def solution(mesh):
    placed = (
        P("dp", ("blk", "uly"), None),
        P("dp", ("blk", "uly"), None),
        P("dp", ("blk", "uly"), None),
        P("dp", "uly", "blk", None),
        P("dp", "uly", "blk"),
        P("dp", None),
        P("dp", ("blk", "uly"), None),
    )
    small = tuple(mesh.shape[axis] for axis in ("uly", "blk", "dp")) == (2, 8, 2)
    return jax.shard_map(
        fused if small else on_device,
        mesh=mesh,
        in_specs=placed,
        out_specs=(
            P("dp", ("blk", "uly"), None),
            P("dp", ("blk", "uly"), None),
            P(("uly", "blk", "dp"), None),
        ),
        check_vma=False,
    )
```

```python
import jax
import jax.numpy as jnp
from jax import lax
from jax.experimental import pallas as pl
from jax.experimental.pallas import tpu as pltpu
from jax.sharding import PartitionSpec as P

MESH = pl.DeviceIdType.MESH
HEAD = 128
HEADS = 8
CHUNK = 128
CHUNKS = 16
SLOTS = 3
GROUP = 8
CORNERS = 4
FIRST, SECOND, THIRD = (1, 2, 3), (4, 5), (6, 7)
HIDDEN = -1e30
LOG2E = 1.4426950408889634


def fused_kernel(
    q_hbm,
    g_hbm,
    kv_hbm,
    o_hbm,
    lse_hbm,
    seg_ref,
    x_hbm,
    dq_ref,
    dkv_ref,
    w_ref,
    qs,
    gs,
    kb,
    vb,
    ob,
    lb,
    p_full,
    p_all,
    ds_all,
    send_kv,
    recv_kv,
    xin,
    vg,
    part,
    part_low,
    part_in,
    q_sem,
    g_sem,
    own_sem,
    x_own_sem,
    kv_send,
    kv_recv,
    o_send,
    o_recv,
    ret_send,
    ret_recv,
    x_send,
    x_recv,
    v_send,
    v_recv,
    p_send,
    p_recv,
):
    rows, head_dim = CHUNK, HEAD
    low, full = jnp.bfloat16, jnp.float32
    uly = lax.axis_index("uly")
    blk = lax.axis_index("blk")
    dp = lax.axis_index("dp")
    chunk = blk * 2 + uly
    half = blk // 4
    member = (blk % 4) * 2 + dp
    corner = uly * 2 + half

    def at_chunk(index):
        index = lax.rem(index + CHUNKS, CHUNKS)
        return {"uly": index % 2, "blk": index // 2, "dp": dp}

    def at_member(index):
        index = lax.rem(index, GROUP)
        return {"uly": uly, "blk": half * 4 + index // 2, "dp": index % 2}

    def at_corner(index):
        index = lax.rem(index, CORNERS)
        return {"uly": index // 2, "blk": (index % 2) * 4 + blk % 4, "dp": dp}

    across = {"uly": 1 - uly, "blk": blk, "dp": dp}

    def cols_of(index, side):
        index = lax.rem(index, GROUP)
        first = (side // 2) * 16 + (side % 2) * 8
        return pl.ds(pl.multiple_of((first + index) * 128, 128), 128)

    def lanes(side):
        return pl.ds(side * 128, 128)

    loads = []
    for h in range(HEADS):
        at_rows, at_cols = pl.ds(h * rows, rows), pl.ds(h * head_dim, head_dim)
        loads.append(pltpu.make_async_copy(q_hbm.at[:, at_cols], qs.at[at_rows], q_sem.at[h]))
        loads.append(pltpu.make_async_copy(g_hbm.at[:, at_cols], gs.at[at_rows], g_sem.at[h]))
    mine = pl.ds(pl.multiple_of(uly * rows, rows), rows)
    theirs = pl.ds(pl.multiple_of((1 - uly) * rows, rows), rows)
    own = pl.ds(0, rows)
    keys_at, values_at = pl.ds(0, head_dim), pl.ds(head_dim, head_dim)
    loads.append(pltpu.make_async_copy(kv_hbm.at[:, keys_at], kb.at[own], own_sem.at[0]))
    loads.append(pltpu.make_async_copy(kv_hbm.at[:, values_at], vb.at[own], own_sem.at[1]))
    loads.append(pltpu.make_async_copy(o_hbm.at[:, mine], ob.at[uly], own_sem.at[2]))
    loads.append(pltpu.make_async_copy(lse_hbm.at[:, mine], lb.at[uly], own_sem.at[3]))
    x_own = [
        pltpu.make_async_copy(
            x_hbm.at[:, cols_of(member, side)], xin.at[0, :, lanes(side)], x_own_sem.at[side]
        )
        for side in range(CORNERS)
    ]

    barrier = pltpu.get_barrier_semaphore()
    for step in (1, 2, -1, -2):
        pl.semaphore_signal(barrier, inc=1, device_id=at_chunk(chunk + step), device_id_type=MESH)
    for k in range(1, CORNERS):
        pl.semaphore_signal(barrier, inc=1, device_id=at_corner(corner + k), device_id_type=MESH)
    for k in range(1, GROUP):
        pl.semaphore_signal(barrier, inc=1, device_id=at_member(member + k), device_id_type=MESH)
    for copy in loads + x_own:
        copy.start()

    lane_query = lax.broadcasted_iota(jnp.int32, (rows, rows), 1)
    row_key = lax.broadcasted_iota(jnp.int32, (rows, rows), 0)

    def seg_row(index):
        index = lax.rem(index + CHUNKS, CHUNKS)
        return seg_ref[:, pl.ds(pl.multiple_of(index * rows, rows), rows)]

    own_seg = jnp.broadcast_to(seg_row(chunk), (rows, rows))
    biases = []
    for s in range(SLOTS):
        key_seg = jnp.broadcast_to(seg_row(chunk - s), (rows, rows)).T
        seen = (key_seg == own_seg) & (chunk >= s)
        if s == 0:
            seen = seen & (row_key <= lane_query)
        biases.append(jnp.where(seen, 0.0, HIDDEN))
    bias = jnp.concatenate(biases, axis=0)
    bias = jnp.concatenate([bias, bias], axis=1)

    pl.semaphore_wait(barrier, GROUP - 1 + CORNERS - 1 + 4)

    def remote(src, dst, send, recv, device):
        return pltpu.make_async_remote_copy(
            src_ref=src,
            dst_ref=dst,
            send_sem=send,
            recv_sem=recv,
            device_id=device,
            device_id_type=MESH,
        )

    def to_chunks(columns, buffer, first):
        return [
            remote(
                kv_hbm.at[:, columns],
                buffer.at[pl.ds(s * rows, rows)],
                kv_send.at[first + s - 1],
                kv_recv.at[first + s - 1],
                at_chunk(chunk + s),
            )
            for s in (1, 2)
        ]

    keys_out = to_chunks(keys_at, kb, 0)
    lse_out = remote(lse_hbm.at[:, theirs], lb.at[uly], o_send.at[1], o_recv.at[1], across)
    values_out = to_chunks(values_at, vb, 2)
    o_out = remote(o_hbm.at[:, theirs], ob.at[uly], o_send.at[0], o_recv.at[0], across)
    early, later = keys_out + [lse_out], values_out + [o_out]
    for copy in early + later:
        copy.start()
    x_out = [
        remote(
            x_hbm.at[:, cols_of(member + k, side)],
            xin.at[k, :, lanes(side)],
            x_send.at[side, k],
            x_recv.at[side, k],
            at_member(member + k),
        )
        for k in range(1, GROUP)
        for side in range(CORNERS)
    ]

    def start_inputs(peers):
        for k in peers:
            for copy in x_out[(k - 1) * CORNERS : k * CORNERS]:
                copy.start()

    start_inputs(FIRST)

    for copy in loads:
        copy.wait()
    for copy in early:
        copy.wait_recv()
    scale = head_dim ** (-0.5)
    across_dims = (((1,), (1,)), ((), ()))
    pairs = [slice(pair * 2 * rows, (pair + 1) * 2 * rows) for pair in range(HEADS // 2)]

    def probs_of(part_rows):
        for pair, at_rows in enumerate(pairs):
            lse = jnp.concatenate(
                [lb[h // 4, h % 4 : h % 4 + 1, :] for h in (2 * pair, 2 * pair + 1)], axis=1
            )
            scores = lax.dot_general(
                kb[part_rows, :], qs[at_rows, :], across_dims, preferred_element_type=full
            )
            prob = jnp.exp2(scores * (scale * LOG2E) - lse * LOG2E + bias[part_rows])
            p_full[part_rows, at_rows] = prob
            p_all[part_rows, at_rows] = prob.astype(low)

    def returned(index):
        return [
            remote(
                send_kv.at[index, s - 1],
                recv_kv.at[index, s - 1],
                ret_send.at[index, s - 1],
                ret_recv.at[index, s - 1],
                at_chunk(chunk - s),
            )
            for s in (1, 2)
        ]

    before, here = slice(rows, SLOTS * rows), slice(0, rows)
    probs_of(before)
    dv = jnp.dot(p_all[before, :], gs[...], preferred_element_type=full)
    send_kv[0] = dv.astype(low).reshape(2, rows, head_dim)
    dv_back = returned(0)
    for copy in dv_back:
        copy.start()
    start_inputs(SECOND)
    probs_of(here)
    dv_own = jnp.dot(p_all[here, :], gs[...], preferred_element_type=full)

    for copy in dv_back:
        copy.wait_recv()
    value_grad = dv_own + recv_kv[0, 0].astype(full) + recv_kv[0, 1].astype(full)
    vg[0] = value_grad.T.astype(low)
    v_out = [
        remote(vg.at[0], vg.at[k], v_send.at[k], v_recv.at[k], at_member(member + k))
        for k in range(1, GROUP)
    ]
    for copy in v_out:
        copy.start()
    start_inputs(THIRD)
    dkv_ref[:, head_dim:] = value_grad.astype(low)

    for copy in later:
        copy.wait_recv()
    for pair, at_rows in enumerate(pairs):
        deltas = []
        for h in (2 * pair, 2 * pair + 1):
            prods = lax.dot_general(
                ob[h // 4, h % 4],
                gs[h * rows : (h + 1) * rows, :],
                across_dims,
                preferred_element_type=full,
            )
            deltas.append(
                jnp.sum(jnp.where(row_key == lane_query, prods, 0.0), axis=0, keepdims=True)
            )
        delta = jnp.concatenate(deltas, axis=1)
        dprob = lax.dot_general(vb[...], gs[at_rows, :], across_dims, preferred_element_type=full)
        ds_all[:, at_rows] = (p_full[:, at_rows] * (dprob - delta)).astype(low)
    dk = jnp.dot(ds_all[before, :], qs[...], preferred_element_type=full) * scale
    send_kv[1] = dk.astype(low).reshape(2, rows, head_dim)
    dk_back = returned(1)
    for copy in dk_back:
        copy.start()

    dk_own = jnp.dot(ds_all[here, :], qs[...], preferred_element_type=full) * scale
    for h in range(HEADS):
        at_rows = slice(h * rows, (h + 1) * rows)
        dq = lax.dot_general(
            ds_all[:, at_rows], kb[...], (((0,), (0,)), ((), ())), preferred_element_type=full
        )
        dq_ref[:, at_rows] = (dq * scale).astype(low)
    for copy in dk_back:
        copy.wait_recv()
    dkv_ref[:, :head_dim] = (
        dk_own + recv_kv[1, 0].astype(full) + recv_kv[1, 1].astype(full)
    ).astype(low)

    for copy in x_own:
        copy.wait()
    total = None
    for first in range(0, GROUP, 2):
        for k in (first, first + 1):
            if k > 0:
                v_out[k - 1].wait_recv()
                for side in range(CORNERS):
                    x_out[(k - 1) * CORNERS + side].wait_recv()
        term = jnp.dot(
            jnp.concatenate([vg[first], vg[first + 1]], axis=1),
            xin[first : first + 2].reshape(2 * rows, CORNERS * 128),
            preferred_element_type=full,
        )
        total = term if total is None else total + term
    for side in range(CORNERS):
        piece = total[:, side * 128 : (side + 1) * 128]
        part[side] = piece
        part_low[side] = piece.astype(low)
    sums = [
        remote(
            part_low.at[lax.rem(corner + k, CORNERS)],
            part_in.at[k],
            p_send.at[k],
            p_recv.at[k],
            at_corner(corner + k),
        )
        for k in range(1, CORNERS)
    ]
    for copy in sums:
        copy.start()

    weight = part[corner]
    for k, copy in enumerate(sums, 1):
        copy.wait_recv()
        weight = weight + part_in[k].astype(full)
    w_ref[...] = weight.T * (rows * CHUNKS * 2) ** (-0.5)
    for copy in early + later + x_out + dv_back + dk_back + v_out + sums:
        copy.wait_send()


def written(dq_ref, dkv_ref, w_ref, dq_out, dkv_out, w_out):
    dq_out[...] = dq_ref[...]
    dkv_out[...] = dkv_ref[...]
    w_out[...] = w_ref[...]


def fused(queries, out_grad, keys_values, attn_output, logsumexp, segments, layer_input):
    anywhere = pl.BlockSpec(memory_space=pl.ANY)
    in_vmem = pl.BlockSpec(memory_space=pltpu.VMEM)
    low, full = jnp.bfloat16, jnp.float32
    dma = pltpu.SemaphoreType.DMA
    width = HEADS * HEAD
    results = (
        jax.ShapeDtypeStruct((CHUNK, width), low),
        jax.ShapeDtypeStruct((CHUNK, 2 * HEAD), low),
        jax.ShapeDtypeStruct((128, HEAD), full),
    )
    found = pl.pallas_call(
        fused_kernel,
        out_shape=results,
        in_specs=[anywhere] * 5 + [in_vmem, anywhere],
        out_specs=(in_vmem, in_vmem, in_vmem),
        scratch_shapes=[
            pltpu.VMEM((width, HEAD), low),
            pltpu.VMEM((width, HEAD), low),
            pltpu.VMEM((SLOTS * CHUNK, HEAD), low),
            pltpu.VMEM((SLOTS * CHUNK, HEAD), low),
            pltpu.VMEM((2, HEADS // 2, CHUNK, HEAD), low),
            pltpu.VMEM((2, HEADS // 2, CHUNK), full),
            pltpu.VMEM((SLOTS * CHUNK, width), full),
            pltpu.VMEM((SLOTS * CHUNK, width), low),
            pltpu.VMEM((SLOTS * CHUNK, width), low),
            pltpu.VMEM((2, 2, CHUNK, HEAD), low),
            pltpu.VMEM((2, 2, CHUNK, HEAD), low),
            pltpu.VMEM((GROUP, CHUNK, CORNERS * 128), low),
            pltpu.VMEM((GROUP, HEAD, CHUNK), low),
            pltpu.VMEM((CORNERS, HEAD, 128), full),
            pltpu.VMEM((CORNERS, HEAD, 128), low),
            pltpu.VMEM((CORNERS, HEAD, 128), low),
            dma((HEADS,)),
            dma((HEADS,)),
            dma((4,)),
            dma((CORNERS,)),
            dma((4,)),
            dma((4,)),
            dma((2,)),
            dma((2,)),
            dma((2, 2)),
            dma((2, 2)),
            dma((CORNERS, GROUP)),
            dma((CORNERS, GROUP)),
            dma((GROUP,)),
            dma((GROUP,)),
            dma((CORNERS,)),
            dma((CORNERS,)),
        ],
        compiler_params=pltpu.CompilerParams(
            collective_id=0, has_side_effects=True, vmem_limit_bytes=60 * 1024 * 1024
        ),
    )(
        queries[0],
        out_grad[0],
        keys_values[0],
        attn_output[0],
        logsumexp[0],
        segments,
        layer_input[0],
    )
    dq, dkv, weight = pl.pallas_call(
        written,
        out_shape=results,
        in_specs=[in_vmem] * 3,
        out_specs=(in_vmem,) * 3,
    )(*found)
    return dq[None], dkv[None], weight


def passed_along(shard, axis, by):
    devices = lax.axis_size(axis)
    pairs = [(i, i + by) for i in range(devices) if 0 <= i + by < devices]
    return lax.ppermute(shard, axis, pairs)


def block_grads(
    query_rows, grad_rows, lse_rows, delta_rows, query_start, key_block, key_start, seq_ids, live
):
    block_rows = query_rows.shape[0]
    local_heads = lse_rows.shape[0]
    head_dim = key_block.shape[1] // 2
    key_rows = key_block.shape[0]
    seq_len = seq_ids.shape[0]
    tile_rows = min(512, block_rows)
    tile_count = block_rows // tile_rows
    scale = head_dim ** (-0.5)
    query_tiles = query_rows.reshape(tile_count, tile_rows, local_heads, head_dim)
    grad_tiles = grad_rows.reshape(tile_count, tile_rows, local_heads, head_dim)
    lse_tiles = lse_rows.reshape(local_heads, tile_count, tile_rows).transpose(1, 0, 2)
    delta_tiles = delta_rows.reshape(local_heads, tile_count, tile_rows).transpose(1, 0, 2)
    keys_part = key_block[:, :head_dim]
    values_part = key_block[:, head_dim:]
    key_pos = key_start + jnp.arange(key_rows, dtype=jnp.int32)
    key_seg = lax.dynamic_slice_in_dim(
        seq_ids, jnp.clip(key_start, 0, seq_len - key_rows), key_rows, 0
    )

    def tile_step(carry, pieces):
        tile_index, query_tile, grad_tile, lse_tile, delta_tile = pieces
        tile_start = query_start + tile_index * tile_rows
        query_pos = tile_start + jnp.arange(tile_rows, dtype=jnp.int32)
        query_seg = lax.dynamic_slice_in_dim(
            seq_ids, jnp.clip(tile_start, 0, seq_len - tile_rows), tile_rows, 0
        )
        visible = (
            live
            & (key_seg[None, :] == query_seg[:, None])
            & (key_pos[None, :] <= query_pos[:, None])
        )
        scores = (
            jnp.einsum("qhd,kd->hqk", query_tile, keys_part, preferred_element_type=jnp.float32)
            * scale
        )
        probs = jnp.where(visible[None], jnp.exp(scores - lse_tile[:, :, None]), 0.0)
        dprobs = jnp.einsum(
            "qhd,kd->hqk", grad_tile, values_part, preferred_element_type=jnp.float32
        )
        dscores = probs * (dprobs - delta_tile[:, :, None])
        probs_low = probs.astype(jnp.bfloat16)
        dscores_low = dscores.astype(jnp.bfloat16)
        query_part = (
            jnp.einsum("hqk,kd->qhd", dscores_low, keys_part, preferred_element_type=jnp.float32)
            * scale
        )
        key_part = (
            jnp.einsum("hqk,qhd->kd", dscores_low, query_tile, preferred_element_type=jnp.float32)
            * scale
        )
        value_part = jnp.einsum(
            "hqk,qhd->kd", probs_low, grad_tile, preferred_element_type=jnp.float32
        )
        query_part, kv_part = (query_part, jnp.concatenate([key_part, value_part], axis=1))
        return (carry + kv_part, query_part)

    start_total = jnp.zeros((key_rows, 2 * head_dim), jnp.float32)
    kv_total, query_parts = lax.scan(
        tile_step,
        start_total,
        (jnp.arange(tile_count, dtype=jnp.int32), query_tiles, grad_tiles, lse_tiles, delta_tiles),
    )
    return (query_parts.reshape(block_rows, local_heads * head_dim), kv_total)


def on_device(queries, out_grad, keys_values, attn_output, logsumexp, segments, layer_input):
    head_dim = keys_values.shape[2] // 2
    query_heads, grad_heads = (
        lax.all_to_all(queries, "uly", split_axis=2, concat_axis=1, tiled=True),
        lax.all_to_all(out_grad, "uly", split_axis=2, concat_axis=1, tiled=True),
    )
    key_block = lax.all_gather(keys_values, "uly", axis=1, tiled=True)[0]
    query_rows = query_heads[0]
    grad_rows = grad_heads[0]
    block_rows = query_rows.shape[0]
    local_heads = attn_output.shape[1]
    lse_rows = logsumexp[0]
    delta_rows = jnp.einsum(
        "thd,htd->ht",
        grad_rows.reshape(block_rows, local_heads, head_dim),
        attn_output[0],
        preferred_element_type=jnp.float32,
    )
    seq_ids = segments[0]
    cycle_index = lax.axis_index("blk")
    own_start = cycle_index * block_rows
    always_live = jnp.asarray(True)
    query_own, kv_own = block_grads(
        query_rows,
        grad_rows,
        lse_rows,
        delta_rows,
        own_start,
        key_block,
        own_start,
        seq_ids,
        always_live,
    )
    key_before = passed_along(key_block, "blk", 1)
    query_before, kv_before = block_grads(
        query_rows,
        grad_rows,
        lse_rows,
        delta_rows,
        own_start,
        key_before,
        own_start - block_rows,
        seq_ids,
        cycle_index >= 1,
    )
    kv_returned = passed_along(kv_before, "blk", -1)
    query_total = query_own + query_before
    kv_total = kv_own + kv_returned
    kv_sums = lax.psum_scatter(kv_total, "uly", scatter_dimension=0, tiled=True)
    kv_grad = kv_sums.astype(jnp.bfloat16)
    query_grad = lax.all_to_all(
        query_total.astype(jnp.bfloat16)[None], "uly", split_axis=1, concat_axis=2, tiled=True
    )
    value_grads = kv_grad[:, head_dim:]
    all_devices = lax.axis_size(("uly", "blk", "dp"))
    total_tokens = layer_input.shape[1] * all_devices
    flat_input = layer_input[0]
    weight_sum = lax.psum_scatter(
        lax.dot_general(
            flat_input, value_grads, (((0,), (0,)), ((), ())), preferred_element_type=jnp.float32
        ),
        ("uly", "blk", "dp"),
        scatter_dimension=0,
        tiled=True,
    )
    return (query_grad, kv_grad[None], weight_sum * total_tokens ** (-0.5))


def solution(mesh):
    placed = (
        P("dp", ("blk", "uly"), None),
        P("dp", ("blk", "uly"), None),
        P("dp", ("blk", "uly"), None),
        P("dp", "uly", "blk", None),
        P("dp", "uly", "blk"),
        P("dp", None),
        P("dp", ("blk", "uly"), None),
    )
    small = tuple(mesh.shape[axis] for axis in ("uly", "blk", "dp")) == (2, 8, 2)
    return jax.shard_map(
        fused if small else on_device,
        mesh=mesh,
        in_specs=placed,
        out_specs=(
            P("dp", ("blk", "uly"), None),
            P("dp", ("blk", "uly"), None),
            P(("uly", "blk", "dp"), None),
        ),
        check_vma=False,
    )
```

```python
import jax
import jax.numpy as jnp
from jax import lax
from jax.experimental import pallas as pl
from jax.experimental.pallas import tpu as pltpu
from jax.sharding import PartitionSpec as P

MESH = pl.DeviceIdType.MESH
HEAD = 128
HEADS = 8
CHUNK = 128
CHUNKS = 16
SLOTS = 3
GROUP = 8
CORNERS = 4
FIRST, SECOND, THIRD = (1, 2, 3), (4, 5), (6, 7)
HIDDEN = -1e30
LOG2E = 1.4426950408889634


def fused_kernel(
    q_hbm,
    g_hbm,
    kv_hbm,
    o_hbm,
    lse_hbm,
    seg_ref,
    x_hbm,
    dq_ref,
    dkv_ref,
    w_ref,
    qs,
    gs,
    kb,
    vb,
    ob,
    lb,
    p_full,
    p_all,
    ds_all,
    send_kv,
    recv_kv,
    xin,
    vg,
    part,
    part_low,
    part_in,
    q_sem,
    g_sem,
    own_sem,
    x_own_sem,
    kv_send,
    kv_recv,
    o_send,
    o_recv,
    ret_send,
    ret_recv,
    x_send,
    x_recv,
    v_send,
    v_recv,
    p_send,
    p_recv,
):
    rows, head_dim = CHUNK, HEAD
    low, full = jnp.bfloat16, jnp.float32
    uly = lax.axis_index("uly")
    blk = lax.axis_index("blk")
    dp = lax.axis_index("dp")
    chunk = blk * 2 + uly
    half = blk // 4
    member = (blk % 4) * 2 + dp
    corner = uly * 2 + half

    def at_chunk(index):
        index = lax.rem(index + CHUNKS, CHUNKS)
        return {"uly": index % 2, "blk": index // 2, "dp": dp}

    def at_member(index):
        index = lax.rem(index, GROUP)
        return {"uly": uly, "blk": half * 4 + index // 2, "dp": index % 2}

    def at_corner(index):
        index = lax.rem(index, CORNERS)
        return {"uly": index // 2, "blk": (index % 2) * 4 + blk % 4, "dp": dp}

    across = {"uly": 1 - uly, "blk": blk, "dp": dp}

    def cols_of(index, side):
        index = lax.rem(index, GROUP)
        first = (side // 2) * 16 + (side % 2) * 8
        return pl.ds(pl.multiple_of((first + index) * 128, 128), 128)

    def lanes(side):
        return pl.ds(side * 128, 128)

    loads = []
    for h in range(HEADS):
        at_rows, at_cols = pl.ds(h * rows, rows), pl.ds(h * head_dim, head_dim)
        loads.append(pltpu.make_async_copy(q_hbm.at[:, at_cols], qs.at[at_rows], q_sem.at[h]))
        loads.append(pltpu.make_async_copy(g_hbm.at[:, at_cols], gs.at[at_rows], g_sem.at[h]))
    mine = pl.ds(pl.multiple_of(uly * rows, rows), rows)
    theirs = pl.ds(pl.multiple_of((1 - uly) * rows, rows), rows)
    own = pl.ds(0, rows)
    keys_at, values_at = pl.ds(0, head_dim), pl.ds(head_dim, head_dim)
    loads.append(pltpu.make_async_copy(kv_hbm.at[:, keys_at], kb.at[own], own_sem.at[0]))
    loads.append(pltpu.make_async_copy(kv_hbm.at[:, values_at], vb.at[own], own_sem.at[1]))
    loads.append(pltpu.make_async_copy(o_hbm.at[:, mine], ob.at[uly], own_sem.at[2]))
    loads.append(pltpu.make_async_copy(lse_hbm.at[:, mine], lb.at[uly], own_sem.at[3]))
    x_own = [
        pltpu.make_async_copy(
            x_hbm.at[:, cols_of(member, side)], xin.at[0, :, lanes(side)], x_own_sem.at[side]
        )
        for side in range(CORNERS)
    ]

    barrier = pltpu.get_barrier_semaphore()
    for step in (1, 2, -1, -2):
        pl.semaphore_signal(barrier, inc=1, device_id=at_chunk(chunk + step), device_id_type=MESH)
    for k in range(1, CORNERS):
        pl.semaphore_signal(barrier, inc=1, device_id=at_corner(corner + k), device_id_type=MESH)
    for k in range(1, GROUP):
        pl.semaphore_signal(barrier, inc=1, device_id=at_member(member + k), device_id_type=MESH)
    for copy in loads + x_own:
        copy.start()

    lane_query = lax.broadcasted_iota(jnp.int32, (rows, rows), 1)
    row_key = lax.broadcasted_iota(jnp.int32, (rows, rows), 0)

    def seg_row(index):
        index = lax.rem(index + CHUNKS, CHUNKS)
        return seg_ref[:, pl.ds(pl.multiple_of(index * rows, rows), rows)]

    own_seg = jnp.broadcast_to(seg_row(chunk), (rows, rows))
    biases = []
    for s in range(SLOTS):
        key_seg = jnp.broadcast_to(seg_row(chunk - s), (rows, rows)).T
        seen = (key_seg == own_seg) & (chunk >= s)
        if s == 0:
            seen = seen & (row_key <= lane_query)
        biases.append(jnp.where(seen, 0.0, HIDDEN))
    bias = jnp.concatenate(biases, axis=0)
    bias = jnp.concatenate([bias, bias], axis=1)

    pl.semaphore_wait(barrier, GROUP - 1 + CORNERS - 1 + 4)

    def remote(src, dst, send, recv, device):
        return pltpu.make_async_remote_copy(
            src_ref=src,
            dst_ref=dst,
            send_sem=send,
            recv_sem=recv,
            device_id=device,
            device_id_type=MESH,
        )

    def to_chunks(columns, buffer, first):
        return [
            remote(
                kv_hbm.at[:, columns],
                buffer.at[pl.ds(s * rows, rows)],
                kv_send.at[first + s - 1],
                kv_recv.at[first + s - 1],
                at_chunk(chunk + s),
            )
            for s in (1, 2)
        ]

    keys_out = to_chunks(keys_at, kb, 0)
    lse_out = remote(lse_hbm.at[:, theirs], lb.at[uly], o_send.at[1], o_recv.at[1], across)
    values_out = to_chunks(values_at, vb, 2)
    o_out = remote(o_hbm.at[:, theirs], ob.at[uly], o_send.at[0], o_recv.at[0], across)
    early, later = keys_out + [lse_out], values_out + [o_out]
    for copy in early + later:
        copy.start()
    x_out = [
        remote(
            x_hbm.at[:, cols_of(member + k, side)],
            xin.at[k, :, lanes(side)],
            x_send.at[side, k],
            x_recv.at[side, k],
            at_member(member + k),
        )
        for k in range(1, GROUP)
        for side in range(CORNERS)
    ]

    def start_inputs(peers):
        for k in peers:
            for copy in x_out[(k - 1) * CORNERS : k * CORNERS]:
                copy.start()

    start_inputs(FIRST)

    for copy in loads:
        copy.wait()
    for copy in early:
        copy.wait_recv()
    scale = head_dim ** (-0.5)
    across_dims = (((1,), (1,)), ((), ()))
    pairs = [slice(pair * 2 * rows, (pair + 1) * 2 * rows) for pair in range(HEADS // 2)]

    def probs_of(part_rows):
        for pair, at_rows in enumerate(pairs):
            lse = jnp.concatenate(
                [lb[h // 4, h % 4 : h % 4 + 1, :] for h in (2 * pair, 2 * pair + 1)], axis=1
            )
            scores = lax.dot_general(
                kb[part_rows, :], qs[at_rows, :], across_dims, preferred_element_type=full
            )
            prob = jnp.exp2(scores * (scale * LOG2E) - lse * LOG2E + bias[part_rows])
            p_full[part_rows, at_rows] = prob
            p_all[part_rows, at_rows] = prob.astype(low)

    def returned(index):
        return [
            remote(
                send_kv.at[index, s - 1],
                recv_kv.at[index, s - 1],
                ret_send.at[index, s - 1],
                ret_recv.at[index, s - 1],
                at_chunk(chunk - s),
            )
            for s in (1, 2)
        ]

    before, here = slice(rows, SLOTS * rows), slice(0, rows)
    probs_of(before)
    dv = jnp.dot(p_all[before, :], gs[...], preferred_element_type=full)
    send_kv[0] = dv.astype(low).reshape(2, rows, head_dim)
    dv_back = returned(0)
    for copy in dv_back:
        copy.start()
    start_inputs(SECOND)
    probs_of(here)
    dv_own = jnp.dot(p_all[here, :], gs[...], preferred_element_type=full)

    for copy in dv_back:
        copy.wait_recv()
    value_grad = dv_own + recv_kv[0, 0].astype(full) + recv_kv[0, 1].astype(full)
    vg[0] = value_grad.T.astype(low)
    v_out = [
        remote(vg.at[0], vg.at[k], v_send.at[k], v_recv.at[k], at_member(member + k))
        for k in range(1, GROUP)
    ]
    for copy in v_out:
        copy.start()
    start_inputs(THIRD)
    dkv_ref[:, head_dim:] = value_grad.astype(low)

    for copy in later:
        copy.wait_recv()
    for pair, at_rows in enumerate(pairs):
        deltas = []
        for h in (2 * pair, 2 * pair + 1):
            prods = lax.dot_general(
                ob[h // 4, h % 4],
                gs[h * rows : (h + 1) * rows, :],
                across_dims,
                preferred_element_type=full,
            )
            deltas.append(
                jnp.sum(jnp.where(row_key == lane_query, prods, 0.0), axis=0, keepdims=True)
            )
        delta = jnp.concatenate(deltas, axis=1)
        dprob = lax.dot_general(vb[...], gs[at_rows, :], across_dims, preferred_element_type=full)
        ds_all[:, at_rows] = (p_full[:, at_rows] * (dprob - delta)).astype(low)
    dk = jnp.dot(ds_all[before, :], qs[...], preferred_element_type=full) * scale
    send_kv[1] = dk.astype(low).reshape(2, rows, head_dim)
    dk_back = returned(1)
    for copy in dk_back:
        copy.start()

    dk_own = jnp.dot(ds_all[here, :], qs[...], preferred_element_type=full) * scale
    for h in range(HEADS):
        at_rows = slice(h * rows, (h + 1) * rows)
        dq = lax.dot_general(
            ds_all[:, at_rows], kb[...], (((0,), (0,)), ((), ())), preferred_element_type=full
        )
        dq_ref[:, at_rows] = (dq * scale).astype(low)
    for copy in x_own:
        copy.wait()
    total = None
    for first in range(0, GROUP, 2):
        for k in (first, first + 1):
            if k > 0:
                v_out[k - 1].wait_recv()
                for side in range(CORNERS):
                    x_out[(k - 1) * CORNERS + side].wait_recv()
        term = jnp.dot(
            jnp.concatenate([vg[first], vg[first + 1]], axis=1),
            xin[first : first + 2].reshape(2 * rows, CORNERS * 128),
            preferred_element_type=full,
        )
        total = term if total is None else total + term
    for side in range(CORNERS):
        piece = total[:, side * 128 : (side + 1) * 128]
        part[side] = piece
        part_low[side] = piece.astype(low)
    sums = [
        remote(
            part_low.at[lax.rem(corner + k, CORNERS)],
            part_in.at[k],
            p_send.at[k],
            p_recv.at[k],
            at_corner(corner + k),
        )
        for k in range(1, CORNERS)
    ]
    for copy in sums:
        copy.start()

    for copy in dk_back:
        copy.wait_recv()
    dkv_ref[:, :head_dim] = (
        dk_own + recv_kv[1, 0].astype(full) + recv_kv[1, 1].astype(full)
    ).astype(low)

    weight = part[corner]
    for k, copy in enumerate(sums, 1):
        copy.wait_recv()
        weight = weight + part_in[k].astype(full)
    w_ref[...] = weight.T * (rows * CHUNKS * 2) ** (-0.5)
    for copy in early + later + x_out + dv_back + dk_back + v_out + sums:
        copy.wait_send()


def written(dq_ref, dkv_ref, w_ref, dq_out, dkv_out, w_out):
    dq_out[...] = dq_ref[...]
    dkv_out[...] = dkv_ref[...]
    w_out[...] = w_ref[...]


def fused(queries, out_grad, keys_values, attn_output, logsumexp, segments, layer_input):
    anywhere = pl.BlockSpec(memory_space=pl.ANY)
    in_vmem = pl.BlockSpec(memory_space=pltpu.VMEM)
    low, full = jnp.bfloat16, jnp.float32
    dma = pltpu.SemaphoreType.DMA
    width = HEADS * HEAD
    results = (
        jax.ShapeDtypeStruct((CHUNK, width), low),
        jax.ShapeDtypeStruct((CHUNK, 2 * HEAD), low),
        jax.ShapeDtypeStruct((128, HEAD), full),
    )
    found = pl.pallas_call(
        fused_kernel,
        out_shape=results,
        in_specs=[anywhere] * 5 + [in_vmem, anywhere],
        out_specs=(in_vmem, in_vmem, in_vmem),
        scratch_shapes=[
            pltpu.VMEM((width, HEAD), low),
            pltpu.VMEM((width, HEAD), low),
            pltpu.VMEM((SLOTS * CHUNK, HEAD), low),
            pltpu.VMEM((SLOTS * CHUNK, HEAD), low),
            pltpu.VMEM((2, HEADS // 2, CHUNK, HEAD), low),
            pltpu.VMEM((2, HEADS // 2, CHUNK), full),
            pltpu.VMEM((SLOTS * CHUNK, width), full),
            pltpu.VMEM((SLOTS * CHUNK, width), low),
            pltpu.VMEM((SLOTS * CHUNK, width), low),
            pltpu.VMEM((2, 2, CHUNK, HEAD), low),
            pltpu.VMEM((2, 2, CHUNK, HEAD), low),
            pltpu.VMEM((GROUP, CHUNK, CORNERS * 128), low),
            pltpu.VMEM((GROUP, HEAD, CHUNK), low),
            pltpu.VMEM((CORNERS, HEAD, 128), full),
            pltpu.VMEM((CORNERS, HEAD, 128), low),
            pltpu.VMEM((CORNERS, HEAD, 128), low),
            dma((HEADS,)),
            dma((HEADS,)),
            dma((4,)),
            dma((CORNERS,)),
            dma((4,)),
            dma((4,)),
            dma((2,)),
            dma((2,)),
            dma((2, 2)),
            dma((2, 2)),
            dma((CORNERS, GROUP)),
            dma((CORNERS, GROUP)),
            dma((GROUP,)),
            dma((GROUP,)),
            dma((CORNERS,)),
            dma((CORNERS,)),
        ],
        compiler_params=pltpu.CompilerParams(
            collective_id=0, has_side_effects=True, vmem_limit_bytes=60 * 1024 * 1024
        ),
    )(
        queries[0],
        out_grad[0],
        keys_values[0],
        attn_output[0],
        logsumexp[0],
        segments,
        layer_input[0],
    )
    dq, dkv, weight = pl.pallas_call(
        written,
        out_shape=results,
        in_specs=[in_vmem] * 3,
        out_specs=(in_vmem,) * 3,
    )(*found)
    return dq[None], dkv[None], weight


def passed_along(shard, axis, by):
    devices = lax.axis_size(axis)
    pairs = [(i, i + by) for i in range(devices) if 0 <= i + by < devices]
    return lax.ppermute(shard, axis, pairs)


def block_grads(
    query_rows, grad_rows, lse_rows, delta_rows, query_start, key_block, key_start, seq_ids, live
):
    block_rows = query_rows.shape[0]
    local_heads = lse_rows.shape[0]
    head_dim = key_block.shape[1] // 2
    key_rows = key_block.shape[0]
    seq_len = seq_ids.shape[0]
    tile_rows = min(512, block_rows)
    tile_count = block_rows // tile_rows
    scale = head_dim ** (-0.5)
    query_tiles = query_rows.reshape(tile_count, tile_rows, local_heads, head_dim)
    grad_tiles = grad_rows.reshape(tile_count, tile_rows, local_heads, head_dim)
    lse_tiles = lse_rows.reshape(local_heads, tile_count, tile_rows).transpose(1, 0, 2)
    delta_tiles = delta_rows.reshape(local_heads, tile_count, tile_rows).transpose(1, 0, 2)
    keys_part = key_block[:, :head_dim]
    values_part = key_block[:, head_dim:]
    key_pos = key_start + jnp.arange(key_rows, dtype=jnp.int32)
    key_seg = lax.dynamic_slice_in_dim(
        seq_ids, jnp.clip(key_start, 0, seq_len - key_rows), key_rows, 0
    )

    def tile_step(carry, pieces):
        tile_index, query_tile, grad_tile, lse_tile, delta_tile = pieces
        tile_start = query_start + tile_index * tile_rows
        query_pos = tile_start + jnp.arange(tile_rows, dtype=jnp.int32)
        query_seg = lax.dynamic_slice_in_dim(
            seq_ids, jnp.clip(tile_start, 0, seq_len - tile_rows), tile_rows, 0
        )
        visible = (
            live
            & (key_seg[None, :] == query_seg[:, None])
            & (key_pos[None, :] <= query_pos[:, None])
        )
        scores = (
            jnp.einsum("qhd,kd->hqk", query_tile, keys_part, preferred_element_type=jnp.float32)
            * scale
        )
        probs = jnp.where(visible[None], jnp.exp(scores - lse_tile[:, :, None]), 0.0)
        dprobs = jnp.einsum(
            "qhd,kd->hqk", grad_tile, values_part, preferred_element_type=jnp.float32
        )
        dscores = probs * (dprobs - delta_tile[:, :, None])
        probs_low = probs.astype(jnp.bfloat16)
        dscores_low = dscores.astype(jnp.bfloat16)
        query_part = (
            jnp.einsum("hqk,kd->qhd", dscores_low, keys_part, preferred_element_type=jnp.float32)
            * scale
        )
        key_part = (
            jnp.einsum("hqk,qhd->kd", dscores_low, query_tile, preferred_element_type=jnp.float32)
            * scale
        )
        value_part = jnp.einsum(
            "hqk,qhd->kd", probs_low, grad_tile, preferred_element_type=jnp.float32
        )
        query_part, kv_part = (query_part, jnp.concatenate([key_part, value_part], axis=1))
        return (carry + kv_part, query_part)

    start_total = jnp.zeros((key_rows, 2 * head_dim), jnp.float32)
    kv_total, query_parts = lax.scan(
        tile_step,
        start_total,
        (jnp.arange(tile_count, dtype=jnp.int32), query_tiles, grad_tiles, lse_tiles, delta_tiles),
    )
    return (query_parts.reshape(block_rows, local_heads * head_dim), kv_total)


def on_device(queries, out_grad, keys_values, attn_output, logsumexp, segments, layer_input):
    head_dim = keys_values.shape[2] // 2
    query_heads, grad_heads = (
        lax.all_to_all(queries, "uly", split_axis=2, concat_axis=1, tiled=True),
        lax.all_to_all(out_grad, "uly", split_axis=2, concat_axis=1, tiled=True),
    )
    key_block = lax.all_gather(keys_values, "uly", axis=1, tiled=True)[0]
    query_rows = query_heads[0]
    grad_rows = grad_heads[0]
    block_rows = query_rows.shape[0]
    local_heads = attn_output.shape[1]
    lse_rows = logsumexp[0]
    delta_rows = jnp.einsum(
        "thd,htd->ht",
        grad_rows.reshape(block_rows, local_heads, head_dim),
        attn_output[0],
        preferred_element_type=jnp.float32,
    )
    seq_ids = segments[0]
    cycle_index = lax.axis_index("blk")
    own_start = cycle_index * block_rows
    always_live = jnp.asarray(True)
    query_own, kv_own = block_grads(
        query_rows,
        grad_rows,
        lse_rows,
        delta_rows,
        own_start,
        key_block,
        own_start,
        seq_ids,
        always_live,
    )
    key_before = passed_along(key_block, "blk", 1)
    query_before, kv_before = block_grads(
        query_rows,
        grad_rows,
        lse_rows,
        delta_rows,
        own_start,
        key_before,
        own_start - block_rows,
        seq_ids,
        cycle_index >= 1,
    )
    kv_returned = passed_along(kv_before, "blk", -1)
    query_total = query_own + query_before
    kv_total = kv_own + kv_returned
    kv_sums = lax.psum_scatter(kv_total, "uly", scatter_dimension=0, tiled=True)
    kv_grad = kv_sums.astype(jnp.bfloat16)
    query_grad = lax.all_to_all(
        query_total.astype(jnp.bfloat16)[None], "uly", split_axis=1, concat_axis=2, tiled=True
    )
    value_grads = kv_grad[:, head_dim:]
    all_devices = lax.axis_size(("uly", "blk", "dp"))
    total_tokens = layer_input.shape[1] * all_devices
    flat_input = layer_input[0]
    weight_sum = lax.psum_scatter(
        lax.dot_general(
            flat_input, value_grads, (((0,), (0,)), ((), ())), preferred_element_type=jnp.float32
        ),
        ("uly", "blk", "dp"),
        scatter_dimension=0,
        tiled=True,
    )
    return (query_grad, kv_grad[None], weight_sum * total_tokens ** (-0.5))


def solution(mesh):
    placed = (
        P("dp", ("blk", "uly"), None),
        P("dp", ("blk", "uly"), None),
        P("dp", ("blk", "uly"), None),
        P("dp", "uly", "blk", None),
        P("dp", "uly", "blk"),
        P("dp", None),
        P("dp", ("blk", "uly"), None),
    )
    small = tuple(mesh.shape[axis] for axis in ("uly", "blk", "dp")) == (2, 8, 2)
    return jax.shard_map(
        fused if small else on_device,
        mesh=mesh,
        in_specs=placed,
        out_specs=(
            P("dp", ("blk", "uly"), None),
            P("dp", ("blk", "uly"), None),
            P(("uly", "blk", "dp"), None),
        ),
        check_vma=False,
    )
```
